32 devices in a mesh: rep: 8 (over y, x, core), shard: 4 (over z).
Axes of the slice: x: 2, y: 2, z: 4, core: 2. Of those that a mesh axis runs over, the one named last changes fastest.
Arguments:
- queries: bfloat16 [4096, 4096], P(('rep', 'shard')), may hold values from -120 to 120
- keys: bfloat16 [4096, 512], P(('rep', 'shard')), may hold values from -5.5 to 5.5
- grad_out: bfloat16 [4096, 4096], P(('rep', 'shard')), may hold values from -3 to 3
- inputs: bfloat16 [4096, 8192], P(('rep', 'shard')), may hold values from -6 to 6
- old_owner: int32 [64], replicated, may hold values from 0 to 2, as said below
- new_owner: int32 [64], replicated, may hold values from 0 to 3, as said below
- param_old: float32 [128, 88, 512], P('rep', 'shard'), may hold values from -0.75 to 0.75
- first_old: float32 [128, 88, 512], P('rep', 'shard'), may hold values from -6 to 6
- second_old: float32 [128, 88, 512], P('rep', 'shard'), may hold values from 0.5 to 20
Outputs:
- param_new: float32 [128, 64, 512], P('rep', 'shard')
- first_new: float32 [128, 64, 512], P('rep', 'shard')
- second_new: float32 [128, 64, 512], P('rep', 'shard')
- weights: bfloat16 [128, 64, 512], P('rep')
The draws below stay inside these ranges and needn't reach their ends.
Inputs may be any that keep to these rules, and one draw needn't show every extreme that they name: `old_owner`: each old owner holds at most 22 blocks, and some hold exactly 22. `new_owner`: each new owner holds exactly 16 blocks.
All inputs are finite; a program needn't handle non-finite values.
Results may differ from the reference program's by a relative error of at most 0.0034.
Values may be sent and summed in bfloat16 or wider, within the bound.
A program may use at most 128 MiB of HBM per device.

```python
import math
import jax
import jax.numpy as jnp
from jax import lax

D = 8192
HEADS = 32
KV = 4
HD = 128
GRP = 8
LENGTH = 512
TOKENS = 4096
BLOCKS = 64
BROWS = 128
OLD = 3
OLD_CAP = 22
NEW_CAP = 16
STEP = 1000
N_SHARD = 4


def paired_draw(key):
    seq_count = TOKENS // LENGTH
    key_values = jnp.clip(jax.random.normal(jax.random.fold_in(key, 11), (seq_count, LENGTH, KV, HD), jnp.float32), -4.5, 4.5)
    query_values = jnp.clip(jax.random.normal(jax.random.fold_in(key, 12), (seq_count, LENGTH, KV, GRP, HD), jnp.float32), -4.5, 4.5)
    return (query_values.reshape(TOKENS, HEADS * HD), key_values.reshape(TOKENS, KV * HD))


def draw_queries(key, part):
    return paired_draw(key)[0].astype(jnp.bfloat16)


def draw_keys(key, part):
    return paired_draw(key)[1].astype(jnp.bfloat16)


def draw_old_owner(key, part):
    shuffled = jax.random.permutation(jax.random.fold_in(key, 21), BLOCKS)
    inverse = jnp.argsort(shuffled)
    return (inverse % OLD).astype(jnp.int32)


def draw_new_owner(key, part):
    shuffled = jax.random.permutation(jax.random.fold_in(key, 22), BLOCKS)
    inverse = jnp.argsort(shuffled)
    return (inverse // NEW_CAP).astype(jnp.int32)


def shard_levels(own_key, shape, split, low, high):
    def one(axis_at, shards_of):
        heights = jax.random.uniform(jax.random.fold_in(jax.random.fold_in(own_key, 6), axis_at), (shards_of,), jnp.float32, low / len(split), high / len(split))
        return jnp.repeat(jnp.exp(heights), shape[axis_at] // shards_of).reshape((-1,) + (1,) * (len(shape) - axis_at - 1))

    level = one(*split[0])
    for cut in split[1:]:
        level = level * one(*cut)
    return level


def centred(own_key, dims, scale, most, shards=(), kind=jnp.bfloat16):
    entries = jax.random.normal(own_key, dims, jnp.float32) * scale
    if len(shards) > 0:
        entries = shard_levels(own_key, dims, shards, -0.22, 0.18) * entries
    return jnp.clip(entries, min=-most, max=most).astype(kind)


def setup_inputs(seed: int = 0) -> dict:
    splits = jax.random.split(jax.random.key(seed), 10)
    return {
        "queries": draw_queries(jax.random.fold_in(splits[9], 71), 0),
        "keys": draw_keys(jax.random.fold_in(splits[9], 71), 0),
        "grad_out": centred(splits[2], (TOKENS, HEADS * HD), (max(TOKENS // 1024, 1)) ** -0.5, 3.0, ((0, 32),)),
        "inputs": centred(splits[3], (TOKENS, D), 1.0, 6.0, ((0, 32),)),
        "old_owner": draw_old_owner(jax.random.fold_in(splits[9], 71), 0),
        "new_owner": draw_new_owner(jax.random.fold_in(splits[9], 71), 0),
        "param_old": centred(splits[6], (BROWS, N_SHARD * OLD_CAP, KV * HD), 0.05, 0.75, ((0, 8), (1, 4)), jnp.float32),
        "first_old": centred(splits[7], (BROWS, N_SHARD * OLD_CAP, KV * HD), 1.0, 6.0, ((0, 8), (1, 4)), jnp.float32),
        "second_old": jnp.clip(jnp.exp(math.log(20.0) - 3.6888795 * jax.random.uniform(splits[8], (BROWS, N_SHARD * OLD_CAP, KV * HD), jnp.float32) ** shard_levels(splits[8], (BROWS, N_SHARD * OLD_CAP, KV * HD), ((0, 8), (1, 4)), -0.2, 0.2)), 0.5, 20.0),
    }


beta_first = 0.9
beta_second = 0.95
learning_rate = 0.02
decay_rate = 0.1
epsilon = 1e-08

def owner_ranks(owner, owners):
    onehot = (owner[:, None] == jnp.arange(owners, dtype=jnp.int32)[None, :]).astype(jnp.int32)
    running = jnp.cumsum(onehot, axis=0)
    return (lax.optimization_barrier(jnp.sum(running * onehot, axis=1)) - 1).astype(jnp.int32)

def adamw(param, first, second, gradient):
    first = beta_first * first + (1.0 - beta_first) * gradient
    second = beta_second * second + (1.0 - beta_second) * gradient * gradient
    first_hat = first / (1.0 - beta_first ** STEP)
    second_hat = second / (1.0 - beta_second ** STEP)
    param = param - learning_rate * (first_hat / (jnp.sqrt(second_hat) + epsilon) + decay_rate * param)
    return (param, first, second)

def group_values(triple):
    query_block, key_block, cotangent = triple
    length = key_block.shape[0]
    scores = jnp.einsum('htd,ud->htu', query_block.astype(jnp.float32), key_block.astype(jnp.float32)) * HD ** (-0.5)
    allowed = jnp.arange(length)[None, :] <= jnp.arange(length)[:, None]
    scores = jnp.where(allowed[None], scores, -jnp.inf)
    highest = lax.optimization_barrier(jnp.max(scores, axis=-1, keepdims=True))
    weights = jnp.exp(scores - highest)
    probs = (weights / lax.optimization_barrier(jnp.sum(weights, axis=-1, keepdims=True))).astype(jnp.bfloat16)
    summed = jnp.einsum('htu,htd->ud', probs.astype(jnp.float32), cotangent.astype(jnp.float32))
    return summed.astype(jnp.bfloat16)

def sequence_values(triple):
    return lax.map(group_values, triple)

def reference(queries, keys, grad_out, inputs, old_owner, new_owner, param_old, first_old, second_old):
    seq_count = TOKENS // LENGTH
    query_groups = queries.reshape(seq_count, LENGTH, KV, GRP, HD).transpose(0, 2, 3, 1, 4)
    cotangent_groups = grad_out.reshape(seq_count, LENGTH, KV, GRP, HD).transpose(0, 2, 3, 1, 4)
    key_groups = keys.reshape(seq_count, LENGTH, KV, HD).transpose(0, 2, 1, 3)
    values = lax.map(sequence_values, (query_groups, key_groups, cotangent_groups))
    values = values.transpose(0, 2, 1, 3).reshape(TOKENS, KV * HD)
    gradient = lax.dot_general(inputs, values, (((0,), (0,)), ((), ())), preferred_element_type=jnp.float32)
    gradient = gradient.reshape(BLOCKS, BROWS, KV * HD).transpose(1, 0, 2)
    old_slot = (old_owner * OLD_CAP + owner_ranks(old_owner, N_SHARD)).astype(jnp.int32)
    param = jnp.take(param_old, old_slot, axis=1)
    first = jnp.take(first_old, old_slot, axis=1)
    second = jnp.take(second_old, old_slot, axis=1)
    param, first, second = adamw(param, first, second, gradient)
    new_slot = (new_owner * NEW_CAP + owner_ranks(new_owner, N_SHARD)).astype(jnp.int32)
    placing = jnp.argsort(new_slot).astype(jnp.int32)
    param_new = jnp.take(param, placing, axis=1)
    first_new = jnp.take(first, placing, axis=1)
    second_new = jnp.take(second, placing, axis=1)
    weights = param.astype(jnp.bfloat16)
    return (param_new, first_new, second_new, weights)
```

```python
import jax
import jax.numpy as jnp
from jax import lax
from jax.experimental import pallas as pl
from jax.experimental.pallas import tpu as pltpu
from jax.sharding import PartitionSpec as P

KV = 4
HD = 128
GRP = 8
STEP = 1000

beta_first = 0.9
beta_second = 0.95
learning_rate = 0.02
decay_rate = 0.1
epsilon = 1e-08


def owner_ranks(owner, owners):
    onehot = (owner[:, None] == jnp.arange(owners, dtype=jnp.int32)[None, :]).astype(jnp.int32)
    running = jnp.cumsum(onehot, axis=0)
    return jnp.sum(running * onehot, axis=1) - 1


def adamw(param, first, second, gradient):
    first = beta_first * first + (1.0 - beta_first) * gradient
    second = beta_second * second + (1.0 - beta_second) * gradient * gradient
    first_hat = first / (1.0 - beta_first**STEP)
    second_hat = second / (1.0 - beta_second**STEP)
    param = param - learning_rate * (
        first_hat / (jnp.sqrt(second_hat) + epsilon) + decay_rate * param
    )
    return (param, first, second)


def value_kernel(where_ref, q_ref, k_ref, g_ref, o_ref):
    me = where_ref[0]
    rows = q_ref.shape[0]
    length = k_ref.shape[0]
    row = lax.broadcasted_iota(jnp.int32, (rows, length), 0)
    col = lax.broadcasted_iota(jnp.int32, (rows, length), 1)
    allowed = col <= jnp.where(col < rows, row, (me + 1) * rows - 1)
    keys = k_ref[...]
    total = jnp.zeros((length, HD), jnp.float32)
    for h in range(GRP):
        span = slice(h * HD, (h + 1) * HD)
        scores = lax.dot_general(
            q_ref[:, span], keys, (((1,), (1,)), ((), ())), preferred_element_type=jnp.float32
        ) * HD ** (-0.5)
        scores = jnp.where(allowed, scores, -jnp.inf)
        highest = jnp.max(scores, axis=-1, keepdims=True)
        weights = jnp.exp(scores - highest)
        probs = (weights / jnp.sum(weights, axis=-1, keepdims=True)).astype(jnp.bfloat16)
        total = total + lax.dot_general(
            probs, g_ref[:, span], (((0,), (0,)), ((), ())), preferred_element_type=jnp.float32
        )
    o_ref[...] = total


def value_terms(me, queries, keys_all, grad_out):
    rows = queries.shape[0]
    length = keys_all.shape[0]
    return pl.pallas_call(
        value_kernel,
        grid=(KV,),
        out_shape=jax.ShapeDtypeStruct((length, KV * HD), jnp.float32),
        in_specs=[
            pl.BlockSpec(memory_space=pltpu.SMEM),
            pl.BlockSpec((rows, GRP * HD), lambda g: (0, g)),
            pl.BlockSpec((length, HD), lambda g: (0, g)),
            pl.BlockSpec((rows, GRP * HD), lambda g: (0, g)),
        ],
        out_specs=pl.BlockSpec((length, HD), lambda g: (0, g)),
        cost_estimate=pl.CostEstimate(
            flops=4 * rows * length * HD * GRP * KV, bytes_accessed=4 << 20, transcendentals=0
        ),
    )(me[None], queries, keys_all, grad_out)


def pick_kernel(block_ref, x_ref, o_ref, p_ref):
    width = HD
    count = o_ref.shape[1] // width

    @pl.loop(0, count)
    def _(i):
        into = pl.ds(pl.multiple_of(i * width, width), width)
        o_ref[:, into] = x_ref[:, pl.ds(pl.multiple_of(block_ref[0, i] * width, width), width)]
        p_ref[:, into] = x_ref[:, pl.ds(pl.multiple_of(block_ref[1, i] * width, width), width)]


def pick(blocks, inputs):
    rows, wide = inputs.shape
    half = jax.ShapeDtypeStruct((rows, wide // 2), inputs.dtype)
    return pl.pallas_call(
        pick_kernel,
        out_shape=(half, half),
        in_specs=[
            pl.BlockSpec(memory_space=pltpu.SMEM),
            pl.BlockSpec(memory_space=pltpu.VMEM),
        ],
        out_specs=(pl.BlockSpec(memory_space=pltpu.VMEM),) * 2,
        cost_estimate=pl.CostEstimate(flops=0, bytes_accessed=4 << 20, transcendentals=0),
    )(blocks, inputs)


def swap(x, axis, size, bit):
    return lax.ppermute(x, axis, [(i, i ^ bit) for i in range(size)])


def halve(x, axis, bit_value):
    mine = lax.dynamic_index_in_dim(x, bit_value, axis, keepdims=False)
    other = lax.dynamic_index_in_dim(x, 1 - bit_value, axis, keepdims=False)
    return mine, other


def spread(onehot, state):
    return jnp.einsum(
        "ns,rsc->rnc",
        onehot.astype(state.dtype),
        state,
        precision=lax.Precision.HIGHEST if state.dtype == jnp.float32 else None,
        preferred_element_type=state.dtype,
    )


def moved_state(state, source_owner, source_rank, me, shards, sources, new_capacity):
    old_capacity = state.shape[1]
    rank_hot = source_rank[:, None] == jnp.arange(old_capacity)[None, :]
    mine = spread(rank_hot & (source_owner == me)[:, None], state)

    def my_part(x, first_shard, count):
        at = jnp.clip(me - first_shard, 0, count - 1) * new_capacity
        part = lax.dynamic_slice_in_dim(x, at, new_capacity, axis=1)
        inside = (me >= first_shard) & (me < first_shard + count)
        return jnp.where(inside, part, jnp.zeros_like(part))

    result = my_part(mine, 0, shards)

    def chain(route):
        out = jnp.zeros_like(result)
        come = None
        for step, (sender, receiver, low, high) in enumerate(route):
            count = high - low
            if step == 0 and old_capacity < count * new_capacity:
                raw = lax.ppermute(state, "shard", [(sender, receiver)])
                come = spread(
                    (rank_hot & (source_owner == sender)[:, None])[
                        low * new_capacity : high * new_capacity
                    ],
                    raw,
                )
            else:
                pay = mine[:, low * new_capacity : high * new_capacity]
                if come is not None:
                    skip = (low - before) * new_capacity
                    pay = pay + come[:, skip : skip + count * new_capacity]
                come = lax.ppermute(pay, "shard", [(sender, receiver)])
            before = low
            here = receiver - low
            part = come[:, here * new_capacity : (here + 1) * new_capacity]
            out = out + jnp.where(me == receiver, part, jnp.zeros_like(part))
        return out

    right = chain([(l, l + 1, l + 1, shards) for l in range(shards - 1)])
    left = chain([(l, l - 1, 0, l) for l in range(sources - 1, 0, -1)])
    return result + right + left


def local(queries, keys, grad_out, inputs, old_owner, new_owner, param_old, first_old, second_old):
    shards = lax.axis_size("shard")
    replicas = lax.axis_size("rep")
    me = lax.axis_index("shard")
    rep = lax.axis_index("rep")
    rows = queries.shape[0]
    blocks = old_owner.shape[0]
    block_rows = inputs.shape[1] // blocks
    own_rows = block_rows // replicas
    new_capacity = blocks // shards
    columns = KV * HD
    sources = shards - shards // 4
    bf16 = jnp.bfloat16

    chunks = [keys]
    for k in range(1, shards):
        chunks.append(lax.ppermute(keys, "shard", [(s, s + k) for s in range(shards - k)]))

    new_slot = new_owner * new_capacity + owner_ranks(new_owner, shards)
    match = new_slot[None, :] == jnp.arange(blocks, dtype=jnp.int32)[:, None]

    def by_slot(table):
        return jnp.sum(jnp.where(match, table[None, :], 0), axis=1)

    new_block = by_slot(jnp.arange(blocks, dtype=jnp.int32))
    source_owner = by_slot(old_owner)
    source_rank = by_slot(owner_ranks(old_owner, shards))

    parity = me % 2
    halves = new_block.reshape(shards // 2, 2, new_capacity).transpose(1, 0, 2).reshape(2, -1)
    mine_first = jnp.where(parity == 0, halves, halves[::-1])
    kept, sent = pick(mine_first, inputs)
    arrived = swap(sent, "shard", shards, 1)

    moved = [
        moved_state(x, source_owner, source_rank, me, shards, sources, new_capacity)
        for x in (first_old.astype(bf16), second_old.astype(bf16), param_old)
    ]
    first, second, param = (x.astype(jnp.float32) for x in moved)

    part = value_terms(me, queries, jnp.concatenate(chunks, axis=0), grad_out)
    values = part[:rows]
    for k in range(1, shards):
        values = values + lax.ppermute(
            part[k * rows : (k + 1) * rows], "shard", [(s, s - k) for s in range(k, shards)]
        )
    values = values.astype(bf16)
    values_pair = swap(values, "shard", shards, 1)

    contract = (((0,), (0,)), ((), ()))
    product = lax.dot_general(
        jnp.concatenate([kept, arrived], axis=0),
        jnp.concatenate([values, values_pair], axis=0),
        contract,
        preferred_element_type=jnp.float32,
    )
    bits = [1 << n for n in range(replicas.bit_length() - 1)]
    split = tuple(2 for _ in bits)
    product = product.reshape((-1,) + split + (own_rows, columns))

    def scatter(x, order):
        left = sorted(order, reverse=True)
        for bit in order:
            mine, other = halve(x, 1 + left.index(bit), (rep // bit) % 2)
            x = mine + swap(other.astype(bf16), "rep", replicas, bit).astype(jnp.float32)
            left.remove(bit)
        return x

    mine, other = halve(product, len(bits), rep % 2)
    product = mine + swap(other.astype(bf16), "rep", replicas, 1).astype(jnp.float32)
    product = product.reshape((2, -1) + product.shape[1:])
    a = scatter(product[0], bits[1:])
    b = scatter(product[1], bits[:0:-1])
    gradient = jnp.concatenate([a, b], axis=0).reshape(
        shards // 2, new_capacity, own_rows, columns
    )
    pair = me // 2
    total = lax.dynamic_index_in_dim(gradient, pair, 0, keepdims=False)
    for k in range(1, shards // 2):
        out = lax.dynamic_index_in_dim(gradient, (pair + k) % (shards // 2), 0, keepdims=False)
        total = total + lax.ppermute(
            out.astype(bf16), "shard", [(s, (s + 2 * k) % shards) for s in range(shards)]
        ).astype(jnp.float32)
    gradient = total.transpose(1, 0, 2)

    param_new, first_new, second_new = adamw(param, first, second, gradient)
    working = param_new.astype(bf16)
    every = [working]
    for k in range(1, shards):
        every.append(
            lax.ppermute(working, "shard", [(s, (s + k) % shards) for s in range(shards)])
        )
    stacked = jnp.concatenate(every, axis=1)
    at = ((me - new_slot // new_capacity) % shards) * new_capacity + new_slot % new_capacity
    weights = spread(at[:, None] == jnp.arange(blocks)[None, :], stacked)
    return (param_new, first_new, second_new, weights)


def fused_kernel(
    hot, q_ref, key_ref, g_ref, x_own, x_out, mom_in, par_in,
    pn_ref, fn_ref, sn_ref, wall,
    kbuf, x_in, part, v_in, v_out, v_pair,
    prod, core_in, keep1, out1, in1, keep2, out2, in2, gown, out3, in3,
    raw_a_mom, raw_a_par, raw_b_mom, raw_b_par,
    a_mom, a_par, b_mom, b_par, r_mom, r_par, l_mom, l_par, st_mom, st_par, grad, w_out,
    k_sem, x_sem, v_sem, vp_sem, c_sem, s1_sem, s2_sem, s3_sem, st_sem, w_sem,
):
    bf16, f32 = jnp.bfloat16, jnp.float32
    me, rep = lax.axis_index("shard"), lax.axis_index("rep")
    shards = kbuf.shape[0]
    rows = key_ref.shape[0]
    length = shards * rows
    sources = shards - shards // 4
    cap = pn_ref.shape[1]
    parts, group = prod.shape[0], prod.shape[1]
    core, xbit, ybit = rep % 2, (rep // 2) % 2, (rep // 4) % 2
    pair = me + 1 - 2 * (me % 2)
    cross = (me + shards // 2) % shards
    rep_core = rep + 1 - 2 * core
    rep_x = rep + 2 - 4 * xbit
    rep_y = rep + 4 - 8 * ybit
    has_left, has_right = me > 0, me < shards - 1

    def send(src, dst, sem, target):
        return pltpu.make_async_remote_copy(
            src_ref=src, dst_ref=dst, send_sem=sem.at[0], recv_sem=sem.at[1],
            device_id=target, device_id_type=pl.DeviceIdType.MESH,
        )

    left, right = (rep, me - 1), (rep, me + 1)

    barrier = pltpu.get_barrier_semaphore()

    def greet(target):
        pl.semaphore_signal(barrier, inc=1, device_id=target, device_id_type=pl.DeviceIdType.MESH)

    for target in ((rep_core, me), (rep_x, me), (rep_y, me), (rep, cross)):
        greet(target)
    pl.when(has_left)(lambda: greet(left))
    pl.when(has_right)(lambda: greet(right))
    pl.semaphore_wait(barrier, 5 + jnp.where(has_left & has_right, 1, 0))

    def key_copy(j):
        src = key_ref if j == 0 else kbuf.at[j]
        return send(src, kbuf.at[j + 1], k_sem.at[j], right)

    own = (mom_in, par_in)
    raw_buf = ((raw_a_mom, raw_a_par), (raw_b_mom, raw_b_par))
    a_buf, b_buf = (a_mom, a_par), (b_mom, b_par)
    r_buf, l_buf = (r_mom, r_par), (l_mom, l_par)
    st_buf = (st_mom, st_par)

    def raw(kind, direction):
        return send(
            own[kind], raw_buf[direction][kind], st_sem.at[kind, direction], (right, left)[direction]
        )

    def raw_send(kind):
        pl.when(me == 0)(lambda: raw(kind, 0).start())
        pl.when(me == sources - 1)(lambda: raw(kind, 1).start())

    pl.when(has_right)(lambda: key_copy(0).start())
    raw_send(0)

    x_copy = send(x_out, x_in, x_sem, (rep, pair))
    x_copy.start()
    raw_send(1)

    kbuf[0] = key_ref[...]
    for j in range(1, shards):
        @pl.when(me >= j)
        def _(j=j):
            key_copy(j - 1).wait_recv()
            if j < shards - 1:
                pl.when(has_right)(lambda: key_copy(j).start())

        @pl.when(me < j)
        def _(j=j):
            kbuf[j] = jnp.zeros(kbuf.shape[1:], kbuf.dtype)

    row = lax.broadcasted_iota(jnp.int32, (rows, length), 0)
    col = lax.broadcasted_iota(jnp.int32, (rows, length), 1)
    allowed = col <= jnp.where(col < rows, row, (me + 1) * rows - 1)

    @pl.loop(0, KV)
    def _(g):
        at = pl.ds(pl.multiple_of(g * HD, HD), HD)
        keys = kbuf[:, :, at].reshape(length, HD)
        total = jnp.zeros((length, HD), f32)
        for h in range(GRP):
            span = pl.ds(pl.multiple_of(g * (GRP * HD) + h * HD, HD), HD)
            scores = lax.dot_general(
                q_ref[:, span], keys, (((1,), (1,)), ((), ())), preferred_element_type=f32
            ) * HD ** (-0.5)
            scores = jnp.where(allowed, scores, -jnp.inf)
            highest = jnp.max(scores, axis=-1, keepdims=True)
            weights = jnp.exp(scores - highest)
            probs = (weights / jnp.sum(weights, axis=-1, keepdims=True)).astype(bf16)
            total = total + lax.dot_general(
                probs, g_ref[:, span], (((0,), (0,)), ((), ())), preferred_element_type=f32
            )
        part[:, :, at] = total.reshape(shards, rows, HD)

    def v_copy(d):
        return send(v_out.at[d], v_in.at[d], v_sem.at[d], left)

    for d in range(shards):
        pl.when((me >= d) & has_right)(lambda d=d: v_copy(d).wait_recv())

        @pl.when((me >= d) & has_right)
        def _(d=d):
            v_out[d] = part[me - d] + v_in[d]

        @pl.when((me >= d) & jnp.logical_not(has_right))
        def _(d=d):
            v_out[d] = part[me - d]

        pl.when(me > d)(lambda d=d: v_copy(d).start())

        @pl.when(me == d)
        def _(d=d):
            v_pair[0] = v_out[d].astype(bf16)

    vp_copy = send(v_pair.at[0], v_pair.at[1], vp_sem, (rep, pair))
    vp_copy.start()

    def select(kind, out, first, count, sources_of, extra=None):
        kinds = own[kind].shape[0]
        tables = []
        for which, _ in sources_of:
            tables.append(hot[which, pl.ds(first, count)].astype(own[kind].dtype))

        @pl.loop(0, own[kind].shape[1])
        def _(r):
            for m in range(kinds):
                total = None
                for table, (_, ref) in zip(tables, sources_of):
                    term = jnp.dot(
                        table, ref[m, r], preferred_element_type=f32,
                        precision=lax.Precision.HIGHEST if kind == 1 else None,
                    )
                    total = term if total is None else total + term
                if extra is not None:
                    total = total + extra(m, r).astype(f32)
                out[m, r] = total.astype(out.dtype)

    def forward_copy(kind, role):
        if role == 0:
            return send(r_buf[kind], a_buf[kind], st_sem.at[kind, 0], right)
        if role == 1:
            return send(l_buf[kind], b_buf[kind], st_sem.at[kind, 1], left)
        return send(l_buf[kind], b_buf[kind], st_sem.at[kind, 0], right)

    def forward(kind):
        @pl.when(me == 1)
        def _():
            raw(kind, 0).wait_recv()
            far = (1, raw_buf[0][kind])
            select(kind, r_buf[kind], 2 * cap, 2 * cap, [(0, own[kind]), far])
            forward_copy(kind, 0).start()
            raw(kind, 1).wait_recv()
            far = (2, raw_buf[1][kind])
            select(kind, l_buf[kind], 0, cap, [(0, own[kind]), far])
            forward_copy(kind, 1).start()

        @pl.when(me == 2)
        def _():
            forward_copy(kind, 0).wait_recv()
            select(
                kind, l_buf[kind], 3 * cap, cap, [(0, own[kind])],
                lambda m, r: a_buf[kind][m, r, pl.ds(cap, cap)],
            )
            forward_copy(kind, 2).start()

    def settle(kind):
        mine = (0, own[kind])

        @pl.when(me == 0)
        def _():
            forward_copy(kind, 1).wait_recv()
            select(kind, st_buf[kind], 0, cap, [mine], lambda m, r: b_buf[kind][m, r])

        @pl.when(me == 1)
        def _():
            far = [(1, raw_buf[0][kind]), (2, raw_buf[1][kind])]
            select(kind, st_buf[kind], cap, cap, [mine] + far)

        @pl.when(me == 2)
        def _():
            select(
                kind, st_buf[kind], 2 * cap, cap, [mine],
                lambda m, r: a_buf[kind][m, r, pl.ds(0, cap)],
            )

        @pl.when(me == 3)
        def _():
            forward_copy(kind, 2).wait_recv()
            select(kind, st_buf[kind], 3 * cap, cap, [mine], lambda m, r: b_buf[kind][m, r])

    vp_copy.wait_recv()
    x_copy.wait_recv()
    contract = (((0,), (0,)), ((), ()))

    def core_copy(n):
        return send(prod.at[n, :, :, :, 1 - core], core_in.at[n], c_sem.at[n], (rep_core, me))

    for n in range(parts):
        @pl.loop(0, group)
        def _(i, n=n):
            at = pl.ds(pl.multiple_of((n * group + i) * HD, HD), HD)
            block = lax.dot_general(x_own[:, at], v_pair[0], contract, preferred_element_type=f32)
            block += lax.dot_general(x_in[:, at], v_pair[1], contract, preferred_element_type=f32)
            prod[n, i] = block.reshape(prod.shape[2:])

        core_copy(n).start()

    forward(0)

    def first_copy(n):
        return send(out1.at[n], in1.at[n], s1_sem.at[n], ((rep_x, rep_y)[n % 2], me))

    def second_copy(n):
        return send(out2.at[n], in2.at[n], s2_sem.at[n], ((rep_y, rep_x)[n % 2], me))

    def cross_copy(n):
        return send(out3.at[n], in3.at[n], s3_sem.at[n], (rep, cross))

    for n in range(parts):
        core_copy(n).wait_recv()

        @pl.loop(0, group)
        def _(i, n=n):
            if n % 2 == 0:
                out1[n, i] = (prod[n, i, :, 1 - xbit, core] + core_in[n, i, :, 1 - xbit]).astype(bf16)
                keep1[n, i] = prod[n, i, :, xbit, core] + core_in[n, i, :, xbit]
            else:
                out1[n, i] = (prod[n, i, 1 - ybit, :, core] + core_in[n, i, 1 - ybit]).astype(bf16)
                keep1[n, i] = prod[n, i, ybit, :, core] + core_in[n, i, ybit]

        first_copy(n).start()

    for n in range(parts):
        first_copy(n).wait_recv()
        bit = (ybit, xbit)[n % 2]

        @pl.loop(0, group)
        def _(i, n=n, bit=bit):
            out2[n, i] = (keep1[n, i, 1 - bit] + in1[n, i, 1 - bit].astype(f32)).astype(bf16)
            keep2[n, i] = keep1[n, i, bit] + in1[n, i, bit].astype(f32)

        second_copy(n).start()

    forward(1)

    half = parts // 2
    for n in range(parts):
        second_copy(n).wait_recv()

        @pl.loop(0, group)
        def _(i, n=n):
            total = keep2[n, i] + in2[n, i].astype(f32)
            if n < half:
                out3[n, i] = total.astype(bf16)
            else:
                gown[n - half, i] = total

        if n < half:
            cross_copy(n).start()

    for kind in range(2):
        settle(kind)

    wrows = wall.shape[1] // half

    def w_copy(n, t, direction):
        origin = (me - t, me + t)[direction]
        ref = wall.at[origin, pl.ds(n * wrows, wrows)]
        src = w_out.at[pl.ds(n * wrows, wrows)] if t == 0 else ref
        return send(src, ref, w_sem.at[n, t, direction], (right, left)[direction])

    for n in range(half):
        cross_copy(n).wait_recv()

        @pl.loop(0, group)
        def _(i, n=n):
            total = gown[n, i] + in3[n, i].astype(f32)
            grad[:, pl.ds(n * group + i, 1), :] = total[:, None, :]

    for n in range(half):
        @pl.loop(n * wrows, (n + 1) * wrows)
        def _(r):
            param, first, second = adamw(
                st_par[0, r], st_mom[0, r].astype(f32), st_mom[1, r].astype(f32), grad[r]
            )
            pn_ref[r] = param
            fn_ref[r] = first
            sn_ref[r] = second
            w_out[r] = param.astype(bf16)
            wall[me, r] = param.astype(bf16)

        pl.when(has_right)(lambda n=n: w_copy(n, 0, 0).start())
        pl.when(has_left)(lambda n=n: w_copy(n, 0, 1).start())

    for t in range(1, shards):
        for n in range(half):
            @pl.when(me >= t)
            def _(n=n, t=t):
                w_in = wall.at[me - t, pl.ds(n * wrows, wrows)]
                send(w_in, w_in, w_sem.at[n, t - 1, 0], right).wait_recv()
                if t < shards - 1:
                    pl.when(has_right)(lambda: w_copy(n, t, 0).start())

            @pl.when(me + t < shards)
            def _(n=n, t=t):
                w_in = wall.at[me + t, pl.ds(n * wrows, wrows)]
                send(w_in, w_in, w_sem.at[n, t - 1, 1], left).wait_recv()
                if t < shards - 1:
                    pl.when(has_left)(lambda: w_copy(n, t, 1).start())

    for j in range(shards - 1):
        pl.when(has_right & (me >= j))(lambda j=j: key_copy(j).wait_send())
    for kind in range(2):
        pl.when(me == 0)(lambda kind=kind: raw(kind, 0).wait_send())
        pl.when(me == sources - 1)(lambda kind=kind: raw(kind, 1).wait_send())
        pl.when(me == 1)(lambda kind=kind: forward_copy(kind, 0).wait_send())
        pl.when(me == 1)(lambda kind=kind: forward_copy(kind, 1).wait_send())
        pl.when(me == 2)(lambda kind=kind: forward_copy(kind, 2).wait_send())
    x_copy.wait_send()
    vp_copy.wait_send()
    for d in range(shards):
        pl.when(me > d)(lambda d=d: v_copy(d).wait_send())
    for n in range(parts):
        core_copy(n).wait_send()
        first_copy(n).wait_send()
        second_copy(n).wait_send()
        if n < half:
            cross_copy(n).wait_send()
    for n in range(half):
        for t in range(shards - 1):
            pl.when(has_right & (me >= t))(lambda n=n, t=t: w_copy(n, t, 0).wait_send())
            pl.when(has_left & (me + t < shards))(lambda n=n, t=t: w_copy(n, t, 1).wait_send())


def fused(queries, keys, grad_out, inputs, old_owner, new_owner, param_old, first_old, second_old):
    shards = lax.axis_size("shard")
    replicas = lax.axis_size("rep")
    me = lax.axis_index("shard")
    rows = queries.shape[0]
    blocks = old_owner.shape[0]
    own_rows = inputs.shape[1] // blocks // replicas
    cap = blocks // shards
    width = KV * HD
    old_cap = param_old.shape[1]
    bf16, f32 = jnp.bfloat16, jnp.float32

    new_slot = new_owner * cap + owner_ranks(new_owner, shards)
    match = new_slot[None, :] == jnp.arange(blocks, dtype=jnp.int32)[:, None]
    old_rank = owner_ranks(old_owner, shards)

    def by_slot(table):
        return jnp.sum(jnp.where(match, table[None, :], 0), axis=1)

    new_block = by_slot(jnp.arange(blocks, dtype=jnp.int32)).reshape(shards, cap)
    owner = by_slot(old_owner)
    rank = by_slot(old_rank)
    rank_hot = rank[:, None] == jnp.arange(old_cap)[None, :]
    hot = jnp.stack(
        [rank_hot & (owner == o)[:, None] for o in (me, 0, shards - shards // 4 - 1)]
    ).astype(f32)
    pair = me + 1 - 2 * (me % 2)

    def blocks_for(s):
        far = (s + shards // 2) % shards
        order = [lax.dynamic_index_in_dim(new_block, o, 0, keepdims=False) for o in (far, s)]
        return jnp.concatenate(order)

    pick_tab = jnp.stack([blocks_for(me), blocks_for(pair)])

    moments = jnp.stack([first_old, second_old]).astype(bf16)
    params = param_old[None]
    kept, sent = pick(pick_tab, inputs)

    parts = 4
    group = 2 * cap // parts
    tile = (own_rows, width)
    slot = jax.ShapeDtypeStruct((own_rows, cap, width), f32)
    V = pltpu.VMEM

    def state(count):
        wide = (own_rows, count, width)
        return [V((2,) + wide, bf16), V((1,) + wide, f32)]

    def dma(*shape):
        return pltpu.SemaphoreType.DMA(shape + (2,))

    outs = pl.pallas_call(
        fused_kernel,
        out_shape=(slot, slot, slot, jax.ShapeDtypeStruct((shards, own_rows, cap, width), bf16)),
        in_specs=[pl.BlockSpec(memory_space=pltpu.VMEM)] * 8,
        out_specs=(pl.BlockSpec(memory_space=pltpu.VMEM),) * 4,
        scratch_shapes=[
            V((shards, rows, width), bf16),
            V(kept.shape, bf16),
            V((shards, rows, width), f32), V((shards, rows, width), f32), V((shards, rows, width), f32),
            V((2, rows, width), bf16),
            V((parts, group, 2, 2, 2) + tile, f32),
            V((parts, group, 2, 2) + tile, f32),
            V((parts, group, 2) + tile, f32),
            V((parts, group, 2) + tile, bf16), V((parts, group, 2) + tile, bf16),
            V((parts, group) + tile, f32),
            V((parts, group) + tile, bf16), V((parts, group) + tile, bf16),
            V((parts // 2, group) + tile, f32),
            V((parts // 2, group) + tile, bf16), V((parts // 2, group) + tile, bf16),
            *state(old_cap), *state(old_cap),
            *state(2 * cap), *state(cap), *state(2 * cap), *state(cap), *state(cap),
            V((own_rows, cap, width), f32),
            V((own_rows, cap, width), bf16),
            dma(shards), dma(), dma(shards), dma(), dma(parts), dma(parts), dma(parts), dma(parts),
            dma(2, 2), dma(parts // 2, shards, 2),
        ],
        compiler_params=pltpu.CompilerParams(
            collective_id=0, has_side_effects=True, vmem_limit_bytes=63 << 20
        ),
    )(hot, queries, keys, grad_out, kept, sent, moments, params)
    every = outs[3].transpose(1, 0, 2, 3).reshape(own_rows, blocks, width)
    weights = spread(new_slot[:, None] == jnp.arange(blocks)[None, :], every)
    return tuple(outs[:3]) + (weights,)


def solution(mesh):
    placed = (
        P(("rep", "shard"), None),
        P(("rep", "shard"), None),
        P(("rep", "shard"), None),
        P(("rep", "shard"), None),
        P(),
        P(),
        P("rep", "shard", None),
        P("rep", "shard", None),
        P("rep", "shard", None),
    )
    small = mesh.shape["shard"] == 4 and mesh.shape["rep"] == 8
    return jax.shard_map(
        fused if small else local,
        mesh=mesh,
        in_specs=placed,
        out_specs=(
            P("rep", "shard", None),
            P("rep", "shard", None),
            P("rep", "shard", None),
            P("rep", None, None),
        ),
        check_vma=False,
    )
```

```python
import jax
import jax.numpy as jnp
from jax import lax
from jax.experimental import pallas as pl
from jax.experimental.pallas import tpu as pltpu
from jax.sharding import PartitionSpec as P

KV = 4
HD = 128
GRP = 8
STEP = 1000

beta_first = 0.9
beta_second = 0.95
learning_rate = 0.02
decay_rate = 0.1
epsilon = 1e-08


def owner_ranks(owner, owners):
    onehot = (owner[:, None] == jnp.arange(owners, dtype=jnp.int32)[None, :]).astype(jnp.int32)
    running = jnp.cumsum(onehot, axis=0)
    return jnp.sum(running * onehot, axis=1) - 1


def adamw(param, first, second, gradient):
    first = beta_first * first + (1.0 - beta_first) * gradient
    second = beta_second * second + (1.0 - beta_second) * gradient * gradient
    first_hat = first / (1.0 - beta_first**STEP)
    second_hat = second / (1.0 - beta_second**STEP)
    param = param - learning_rate * (
        first_hat / (jnp.sqrt(second_hat) + epsilon) + decay_rate * param
    )
    return (param, first, second)


def value_kernel(where_ref, q_ref, k_ref, g_ref, o_ref):
    me = where_ref[0]
    rows = q_ref.shape[0]
    length = k_ref.shape[0]
    row = lax.broadcasted_iota(jnp.int32, (rows, length), 0)
    col = lax.broadcasted_iota(jnp.int32, (rows, length), 1)
    allowed = col <= jnp.where(col < rows, row, (me + 1) * rows - 1)
    keys = k_ref[...]
    total = jnp.zeros((length, HD), jnp.float32)
    for h in range(GRP):
        span = slice(h * HD, (h + 1) * HD)
        scores = lax.dot_general(
            q_ref[:, span], keys, (((1,), (1,)), ((), ())), preferred_element_type=jnp.float32
        ) * HD ** (-0.5)
        scores = jnp.where(allowed, scores, -jnp.inf)
        highest = jnp.max(scores, axis=-1, keepdims=True)
        weights = jnp.exp(scores - highest)
        probs = (weights / jnp.sum(weights, axis=-1, keepdims=True)).astype(jnp.bfloat16)
        total = total + lax.dot_general(
            probs, g_ref[:, span], (((0,), (0,)), ((), ())), preferred_element_type=jnp.float32
        )
    o_ref[...] = total


def value_terms(me, queries, keys_all, grad_out):
    rows = queries.shape[0]
    length = keys_all.shape[0]
    return pl.pallas_call(
        value_kernel,
        grid=(KV,),
        out_shape=jax.ShapeDtypeStruct((length, KV * HD), jnp.float32),
        in_specs=[
            pl.BlockSpec(memory_space=pltpu.SMEM),
            pl.BlockSpec((rows, GRP * HD), lambda g: (0, g)),
            pl.BlockSpec((length, HD), lambda g: (0, g)),
            pl.BlockSpec((rows, GRP * HD), lambda g: (0, g)),
        ],
        out_specs=pl.BlockSpec((length, HD), lambda g: (0, g)),
        cost_estimate=pl.CostEstimate(
            flops=4 * rows * length * HD * GRP * KV, bytes_accessed=4 << 20, transcendentals=0
        ),
    )(me[None], queries, keys_all, grad_out)


def pick_kernel(block_ref, x_ref, o_ref, p_ref):
    width = HD
    count = o_ref.shape[1] // width

    @pl.loop(0, count)
    def _(i):
        into = pl.ds(pl.multiple_of(i * width, width), width)
        o_ref[:, into] = x_ref[:, pl.ds(pl.multiple_of(block_ref[0, i] * width, width), width)]
        p_ref[:, into] = x_ref[:, pl.ds(pl.multiple_of(block_ref[1, i] * width, width), width)]


def pick(blocks, inputs):
    rows, wide = inputs.shape
    half = jax.ShapeDtypeStruct((rows, wide // 2), inputs.dtype)
    return pl.pallas_call(
        pick_kernel,
        out_shape=(half, half),
        in_specs=[
            pl.BlockSpec(memory_space=pltpu.SMEM),
            pl.BlockSpec(memory_space=pltpu.VMEM),
        ],
        out_specs=(pl.BlockSpec(memory_space=pltpu.VMEM),) * 2,
        cost_estimate=pl.CostEstimate(flops=0, bytes_accessed=4 << 20, transcendentals=0),
    )(blocks, inputs)


def swap(x, axis, size, bit):
    return lax.ppermute(x, axis, [(i, i ^ bit) for i in range(size)])


def halve(x, axis, bit_value):
    mine = lax.dynamic_index_in_dim(x, bit_value, axis, keepdims=False)
    other = lax.dynamic_index_in_dim(x, 1 - bit_value, axis, keepdims=False)
    return mine, other


def spread(onehot, state):
    return jnp.einsum(
        "ns,rsc->rnc",
        onehot.astype(state.dtype),
        state,
        precision=lax.Precision.HIGHEST if state.dtype == jnp.float32 else None,
        preferred_element_type=state.dtype,
    )


def moved_state(state, source_owner, source_rank, me, shards, sources, new_capacity):
    old_capacity = state.shape[1]
    rank_hot = source_rank[:, None] == jnp.arange(old_capacity)[None, :]
    mine = spread(rank_hot & (source_owner == me)[:, None], state)

    def my_part(x, first_shard, count):
        at = jnp.clip(me - first_shard, 0, count - 1) * new_capacity
        part = lax.dynamic_slice_in_dim(x, at, new_capacity, axis=1)
        inside = (me >= first_shard) & (me < first_shard + count)
        return jnp.where(inside, part, jnp.zeros_like(part))

    result = my_part(mine, 0, shards)

    def chain(route):
        out = jnp.zeros_like(result)
        come = None
        for step, (sender, receiver, low, high) in enumerate(route):
            count = high - low
            if step == 0 and old_capacity < count * new_capacity:
                raw = lax.ppermute(state, "shard", [(sender, receiver)])
                come = spread(
                    (rank_hot & (source_owner == sender)[:, None])[
                        low * new_capacity : high * new_capacity
                    ],
                    raw,
                )
            else:
                pay = mine[:, low * new_capacity : high * new_capacity]
                if come is not None:
                    skip = (low - before) * new_capacity
                    pay = pay + come[:, skip : skip + count * new_capacity]
                come = lax.ppermute(pay, "shard", [(sender, receiver)])
            before = low
            here = receiver - low
            part = come[:, here * new_capacity : (here + 1) * new_capacity]
            out = out + jnp.where(me == receiver, part, jnp.zeros_like(part))
        return out

    right = chain([(l, l + 1, l + 1, shards) for l in range(shards - 1)])
    left = chain([(l, l - 1, 0, l) for l in range(sources - 1, 0, -1)])
    return result + right + left


def local(queries, keys, grad_out, inputs, old_owner, new_owner, param_old, first_old, second_old):
    shards = lax.axis_size("shard")
    replicas = lax.axis_size("rep")
    me = lax.axis_index("shard")
    rep = lax.axis_index("rep")
    rows = queries.shape[0]
    blocks = old_owner.shape[0]
    block_rows = inputs.shape[1] // blocks
    own_rows = block_rows // replicas
    new_capacity = blocks // shards
    columns = KV * HD
    sources = shards - shards // 4
    bf16 = jnp.bfloat16

    chunks = [keys]
    for k in range(1, shards):
        chunks.append(lax.ppermute(keys, "shard", [(s, s + k) for s in range(shards - k)]))

    new_slot = new_owner * new_capacity + owner_ranks(new_owner, shards)
    match = new_slot[None, :] == jnp.arange(blocks, dtype=jnp.int32)[:, None]

    def by_slot(table):
        return jnp.sum(jnp.where(match, table[None, :], 0), axis=1)

    new_block = by_slot(jnp.arange(blocks, dtype=jnp.int32))
    source_owner = by_slot(old_owner)
    source_rank = by_slot(owner_ranks(old_owner, shards))

    parity = me % 2
    halves = new_block.reshape(shards // 2, 2, new_capacity).transpose(1, 0, 2).reshape(2, -1)
    mine_first = jnp.where(parity == 0, halves, halves[::-1])
    kept, sent = pick(mine_first, inputs)
    arrived = swap(sent, "shard", shards, 1)

    moved = [
        moved_state(x, source_owner, source_rank, me, shards, sources, new_capacity)
        for x in (first_old.astype(bf16), second_old.astype(bf16), param_old)
    ]
    first, second, param = (x.astype(jnp.float32) for x in moved)

    part = value_terms(me, queries, jnp.concatenate(chunks, axis=0), grad_out)
    values = part[:rows]
    for k in range(1, shards):
        values = values + lax.ppermute(
            part[k * rows : (k + 1) * rows], "shard", [(s, s - k) for s in range(k, shards)]
        )
    values = values.astype(bf16)
    values_pair = swap(values, "shard", shards, 1)

    contract = (((0,), (0,)), ((), ()))
    product = lax.dot_general(
        jnp.concatenate([kept, arrived], axis=0),
        jnp.concatenate([values, values_pair], axis=0),
        contract,
        preferred_element_type=jnp.float32,
    )
    bits = [1 << n for n in range(replicas.bit_length() - 1)]
    split = tuple(2 for _ in bits)
    product = product.reshape((-1,) + split + (own_rows, columns))

    def scatter(x, order):
        left = sorted(order, reverse=True)
        for bit in order:
            mine, other = halve(x, 1 + left.index(bit), (rep // bit) % 2)
            x = mine + swap(other.astype(bf16), "rep", replicas, bit).astype(jnp.float32)
            left.remove(bit)
        return x

    mine, other = halve(product, len(bits), rep % 2)
    product = mine + swap(other.astype(bf16), "rep", replicas, 1).astype(jnp.float32)
    product = product.reshape((2, -1) + product.shape[1:])
    a = scatter(product[0], bits[1:])
    b = scatter(product[1], bits[:0:-1])
    gradient = jnp.concatenate([a, b], axis=0).reshape(
        shards // 2, new_capacity, own_rows, columns
    )
    pair = me // 2
    total = lax.dynamic_index_in_dim(gradient, pair, 0, keepdims=False)
    for k in range(1, shards // 2):
        out = lax.dynamic_index_in_dim(gradient, (pair + k) % (shards // 2), 0, keepdims=False)
        total = total + lax.ppermute(
            out.astype(bf16), "shard", [(s, (s + 2 * k) % shards) for s in range(shards)]
        ).astype(jnp.float32)
    gradient = total.transpose(1, 0, 2)

    param_new, first_new, second_new = adamw(param, first, second, gradient)
    working = param_new.astype(bf16)
    every = [working]
    for k in range(1, shards):
        every.append(
            lax.ppermute(working, "shard", [(s, (s + k) % shards) for s in range(shards)])
        )
    stacked = jnp.concatenate(every, axis=1)
    at = ((me - new_slot // new_capacity) % shards) * new_capacity + new_slot % new_capacity
    weights = spread(at[:, None] == jnp.arange(blocks)[None, :], stacked)
    return (param_new, first_new, second_new, weights)


def fused_kernel(
    hot, q_ref, key_ref, g_ref, x_own, x_out, mom_in, par_in, par_full,
    pn_ref, fn_ref, sn_ref, wall,
    kbuf, x_in, part, v_in, v_out, v_pair,
    prod, core_in, keep1, out1, in1, keep2, out2, in2, gown, out3, in3,
    raw_a_mom, raw_a_par, raw_b_mom, raw_b_par,
    a_mom, a_par, b_mom, b_par, r_mom, r_par, l_mom, l_par, st_mom, st_par, grad, w_out,
    k_sem, x_sem, v_sem, vp_sem, c_sem, s1_sem, s2_sem, s3_sem, st_sem, w_sem,
):
    bf16, f32 = jnp.bfloat16, jnp.float32
    me, rep = lax.axis_index("shard"), lax.axis_index("rep")
    shards = kbuf.shape[0]
    rows = key_ref.shape[0]
    length = shards * rows
    sources = shards - shards // 4
    cap = pn_ref.shape[1]
    parts, group = prod.shape[0], prod.shape[1]
    core, xbit, ybit = rep % 2, (rep // 2) % 2, (rep // 4) % 2
    pair = me + 1 - 2 * (me % 2)
    cross = (me + shards // 2) % shards
    rep_core = rep + 1 - 2 * core
    rep_x = rep + 2 - 4 * xbit
    rep_y = rep + 4 - 8 * ybit
    has_left, has_right = me > 0, me < shards - 1

    def send(src, dst, sem, target):
        return pltpu.make_async_remote_copy(
            src_ref=src, dst_ref=dst, send_sem=sem.at[0], recv_sem=sem.at[1],
            device_id=target, device_id_type=pl.DeviceIdType.MESH,
        )

    left, right = (rep, me - 1), (rep, me + 1)

    barrier = pltpu.get_barrier_semaphore()

    def greet(target):
        pl.semaphore_signal(barrier, inc=1, device_id=target, device_id_type=pl.DeviceIdType.MESH)

    for target in ((rep_core, me), (rep_x, me), (rep_y, me), (rep, cross)):
        greet(target)
    pl.when(has_left)(lambda: greet(left))
    pl.when(has_right)(lambda: greet(right))
    pl.semaphore_wait(barrier, 5 + jnp.where(has_left & has_right, 1, 0))

    def key_copy(j):
        src = key_ref if j == 0 else kbuf.at[j]
        return send(src, kbuf.at[j + 1], k_sem.at[j], right)

    own = (mom_in, par_in)
    raw_buf = ((raw_a_mom, raw_a_par), (raw_b_mom, raw_b_par))
    a_buf, b_buf = (a_mom, a_par), (b_mom, b_par)
    r_buf, l_buf = (r_mom, r_par), (l_mom, l_par)
    st_buf = (st_mom, st_par)

    def raw(kind, direction):
        return send(
            own[kind], raw_buf[direction][kind], st_sem.at[kind, direction], (right, left)[direction]
        )

    def raw_send(kind):
        pl.when(me == 0)(lambda: raw(kind, 0).start())
        pl.when(me == sources - 1)(lambda: raw(kind, 1).start())

    pl.when(has_right)(lambda: key_copy(0).start())
    raw_send(0)

    x_copy = send(x_out, x_in, x_sem, (rep, pair))
    x_copy.start()

    kbuf[0] = key_ref[...]
    for j in range(1, shards):
        @pl.when(me >= j)
        def _(j=j):
            key_copy(j - 1).wait_recv()
            if j < shards - 1:
                pl.when(has_right)(lambda: key_copy(j).start())

        @pl.when(me < j)
        def _(j=j):
            kbuf[j] = jnp.zeros(kbuf.shape[1:], kbuf.dtype)

    row = lax.broadcasted_iota(jnp.int32, (rows, length), 0)
    col = lax.broadcasted_iota(jnp.int32, (rows, length), 1)
    allowed = col <= jnp.where(col < rows, row, (me + 1) * rows - 1)

    @pl.loop(0, KV)
    def _(g):
        at = pl.ds(pl.multiple_of(g * HD, HD), HD)
        keys = kbuf[:, :, at].reshape(length, HD)
        total = jnp.zeros((length, HD), f32)
        for h in range(GRP):
            span = pl.ds(pl.multiple_of(g * (GRP * HD) + h * HD, HD), HD)
            scores = lax.dot_general(
                q_ref[:, span], keys, (((1,), (1,)), ((), ())), preferred_element_type=f32
            ) * HD ** (-0.5)
            scores = jnp.where(allowed, scores, -jnp.inf)
            highest = jnp.max(scores, axis=-1, keepdims=True)
            weights = jnp.exp(scores - highest)
            probs = (weights / jnp.sum(weights, axis=-1, keepdims=True)).astype(bf16)
            total = total + lax.dot_general(
                probs, g_ref[:, span], (((0,), (0,)), ((), ())), preferred_element_type=f32
            )
        part[:, :, at] = total.reshape(shards, rows, HD)

    def select(kind, out, first, count, sources_of, extra=None):
        kinds = own[kind].shape[0]
        tables = []
        for which, ref in sources_of:
            tables.append(hot[which, pl.ds(first, count)].astype(ref.dtype))

        @pl.loop(0, own[kind].shape[1])
        def _(r):
            for m in range(kinds):
                total = None
                for table, (_, ref) in zip(tables, sources_of):
                    term = jnp.dot(
                        table, ref[m, r], preferred_element_type=f32,
                        precision=lax.Precision.HIGHEST if ref.dtype == f32 else None,
                    )
                    total = term if total is None else total + term
                if extra is not None:
                    total = total + extra(m, r).astype(f32)
                out[m, r] = total.astype(out.dtype)

    def forward_copy(kind, role):
        if role == 0:
            return send(r_buf[kind], a_buf[kind], st_sem.at[kind, 0], right)
        if role == 1:
            return send(l_buf[kind], b_buf[kind], st_sem.at[kind, 1], left)
        return send(l_buf[kind], b_buf[kind], st_sem.at[kind, 0], right)

    def forward_right(kind):
        @pl.when(me == 1)
        def _():
            raw(kind, 0).wait_recv()
            far = (1, raw_buf[0][kind])
            select(kind, r_buf[kind], 2 * cap, 2 * cap, [(0, own[kind]), far])
            forward_copy(kind, 0).start()

    def forward_left(kind):
        @pl.when(me == 1)
        def _():
            raw(kind, 1).wait_recv()
            far = (2, raw_buf[1][kind])
            select(kind, l_buf[kind], 0, cap, [(0, own[kind]), far])
            forward_copy(kind, 1).start()

    def forward_last(kind):
        @pl.when(me == 2)
        def _():
            forward_copy(kind, 0).wait_recv()
            select(
                kind, l_buf[kind], 3 * cap, cap, [(0, own[kind])],
                lambda m, r: a_buf[kind][m, r, pl.ds(cap, cap)],
            )
            forward_copy(kind, 2).start()

    forward_right(0)

    def v_copy(d):
        return send(v_out.at[d], v_in.at[d], v_sem.at[d], left)

    for d in range(shards):
        pl.when((me >= d) & has_right)(lambda d=d: v_copy(d).wait_recv())

        @pl.when((me >= d) & has_right)
        def _(d=d):
            v_out[d] = part[me - d] + v_in[d]

        @pl.when((me >= d) & jnp.logical_not(has_right))
        def _(d=d):
            v_out[d] = part[me - d]

        pl.when(me > d)(lambda d=d: v_copy(d).start())

        @pl.when(me == d)
        def _(d=d):
            v_pair[0] = v_out[d].astype(bf16)

    vp_copy = send(v_pair.at[0], v_pair.at[1], vp_sem, (rep, pair))
    vp_copy.start()
    raw_send(1)

    def settle(kind):
        mine = (0, (mom_in, par_full)[kind])

        @pl.when(me == 0)
        def _():
            forward_copy(kind, 1).wait_recv()
            select(kind, st_buf[kind], 0, cap, [mine], lambda m, r: b_buf[kind][m, r])

        @pl.when(me == 1)
        def _():
            far = [(1, raw_buf[0][kind]), (2, raw_buf[1][kind])]
            select(kind, st_buf[kind], cap, cap, [mine] + far)

        @pl.when(me == 2)
        def _():
            select(
                kind, st_buf[kind], 2 * cap, cap, [mine],
                lambda m, r: a_buf[kind][m, r, pl.ds(0, cap)],
            )

        @pl.when(me == 3)
        def _():
            forward_copy(kind, 2).wait_recv()
            select(kind, st_buf[kind], 3 * cap, cap, [mine], lambda m, r: b_buf[kind][m, r])

    vp_copy.wait_recv()
    x_copy.wait_recv()
    contract = (((0,), (0,)), ((), ()))

    def core_copy(n):
        return send(prod.at[n, :, :, :, 1 - core], core_in.at[n], c_sem.at[n], (rep_core, me))

    for n in range(parts):
        @pl.loop(0, group)
        def _(i, n=n):
            at = pl.ds(pl.multiple_of((n * group + i) * HD, HD), HD)
            block = lax.dot_general(x_own[:, at], v_pair[0], contract, preferred_element_type=f32)
            block += lax.dot_general(x_in[:, at], v_pair[1], contract, preferred_element_type=f32)
            prod[n, i] = block.reshape(prod.shape[2:])

        core_copy(n).start()

    forward_left(0)

    def first_copy(n):
        return send(out1.at[n], in1.at[n], s1_sem.at[n], ((rep_x, rep_y)[n % 2], me))

    def second_copy(n):
        return send(out2.at[n], in2.at[n], s2_sem.at[n], ((rep_y, rep_x)[n % 2], me))

    def cross_copy(n):
        return send(out3.at[n], in3.at[n], s3_sem.at[n], (rep, cross))

    for n in range(parts):
        core_copy(n).wait_recv()

        @pl.loop(0, group)
        def _(i, n=n):
            if n % 2 == 0:
                out1[n, i] = (prod[n, i, :, 1 - xbit, core] + core_in[n, i, :, 1 - xbit]).astype(bf16)
                keep1[n, i] = prod[n, i, :, xbit, core] + core_in[n, i, :, xbit]
            else:
                out1[n, i] = (prod[n, i, 1 - ybit, :, core] + core_in[n, i, 1 - ybit]).astype(bf16)
                keep1[n, i] = prod[n, i, ybit, :, core] + core_in[n, i, ybit]

        first_copy(n).start()

    forward_right(1)
    forward_last(0)

    for n in range(parts):
        first_copy(n).wait_recv()
        bit = (ybit, xbit)[n % 2]

        @pl.loop(0, group)
        def _(i, n=n, bit=bit):
            out2[n, i] = (keep1[n, i, 1 - bit] + in1[n, i, 1 - bit].astype(f32)).astype(bf16)
            keep2[n, i] = keep1[n, i, bit] + in1[n, i, bit].astype(f32)

        second_copy(n).start()

    forward_left(1)
    forward_last(1)

    half = parts // 2
    for n in range(parts):
        second_copy(n).wait_recv()

        @pl.loop(0, group)
        def _(i, n=n):
            total = keep2[n, i] + in2[n, i].astype(f32)
            if n < half:
                out3[n, i] = total.astype(bf16)
            else:
                gown[n - half, i] = total

        if n < half:
            cross_copy(n).start()

    for kind in range(2):
        settle(kind)

    wrows = wall.shape[1] // half

    def w_copy(n, t, direction):
        origin = (me - t, me + t)[direction]
        ref = wall.at[origin, pl.ds(n * wrows, wrows)]
        src = w_out.at[pl.ds(n * wrows, wrows)] if t == 0 else ref
        return send(src, ref, w_sem.at[n, t, direction], (right, left)[direction])

    for n in range(half):
        cross_copy(n).wait_recv()

        @pl.loop(0, group)
        def _(i, n=n):
            total = gown[n, i] + in3[n, i].astype(f32)
            grad[:, pl.ds(n * group + i, 1), :] = total[:, None, :]

    for n in range(half):
        @pl.loop(n * wrows, (n + 1) * wrows)
        def _(r):
            param, first, second = adamw(
                st_par[0, r], st_mom[0, r].astype(f32), st_mom[1, r].astype(f32), grad[r]
            )
            pn_ref[r] = param
            fn_ref[r] = first
            sn_ref[r] = second
            w_out[r] = param.astype(bf16)
            wall[me, r] = param.astype(bf16)

        pl.when(has_right)(lambda n=n: w_copy(n, 0, 0).start())
        pl.when(has_left)(lambda n=n: w_copy(n, 0, 1).start())

    for t in range(1, shards):
        for n in range(half):
            @pl.when(me >= t)
            def _(n=n, t=t):
                w_in = wall.at[me - t, pl.ds(n * wrows, wrows)]
                send(w_in, w_in, w_sem.at[n, t - 1, 0], right).wait_recv()
                if t < shards - 1:
                    pl.when(has_right)(lambda: w_copy(n, t, 0).start())

            @pl.when(me + t < shards)
            def _(n=n, t=t):
                w_in = wall.at[me + t, pl.ds(n * wrows, wrows)]
                send(w_in, w_in, w_sem.at[n, t - 1, 1], left).wait_recv()
                if t < shards - 1:
                    pl.when(has_left)(lambda: w_copy(n, t, 1).start())

    for j in range(shards - 1):
        pl.when(has_right & (me >= j))(lambda j=j: key_copy(j).wait_send())
    for kind in range(2):
        pl.when(me == 0)(lambda kind=kind: raw(kind, 0).wait_send())
        pl.when(me == sources - 1)(lambda kind=kind: raw(kind, 1).wait_send())
        pl.when(me == 1)(lambda kind=kind: forward_copy(kind, 0).wait_send())
        pl.when(me == 1)(lambda kind=kind: forward_copy(kind, 1).wait_send())
        pl.when(me == 2)(lambda kind=kind: forward_copy(kind, 2).wait_send())
    x_copy.wait_send()
    vp_copy.wait_send()
    for d in range(shards):
        pl.when(me > d)(lambda d=d: v_copy(d).wait_send())
    for n in range(parts):
        core_copy(n).wait_send()
        first_copy(n).wait_send()
        second_copy(n).wait_send()
        if n < half:
            cross_copy(n).wait_send()
    for n in range(half):
        for t in range(shards - 1):
            pl.when(has_right & (me >= t))(lambda n=n, t=t: w_copy(n, t, 0).wait_send())
            pl.when(has_left & (me + t < shards))(lambda n=n, t=t: w_copy(n, t, 1).wait_send())


def fused(queries, keys, grad_out, inputs, old_owner, new_owner, param_old, first_old, second_old):
    shards = lax.axis_size("shard")
    replicas = lax.axis_size("rep")
    me = lax.axis_index("shard")
    rows = queries.shape[0]
    blocks = old_owner.shape[0]
    own_rows = inputs.shape[1] // blocks // replicas
    cap = blocks // shards
    width = KV * HD
    old_cap = param_old.shape[1]
    bf16, f32 = jnp.bfloat16, jnp.float32

    new_slot = new_owner * cap + owner_ranks(new_owner, shards)
    match = new_slot[None, :] == jnp.arange(blocks, dtype=jnp.int32)[:, None]
    old_rank = owner_ranks(old_owner, shards)

    def by_slot(table):
        return jnp.sum(jnp.where(match, table[None, :], 0), axis=1)

    new_block = by_slot(jnp.arange(blocks, dtype=jnp.int32)).reshape(shards, cap)
    owner = by_slot(old_owner)
    rank = by_slot(old_rank)
    rank_hot = rank[:, None] == jnp.arange(old_cap)[None, :]
    hot = jnp.stack(
        [rank_hot & (owner == o)[:, None] for o in (me, 0, shards - shards // 4 - 1)]
    ).astype(f32)
    pair = me + 1 - 2 * (me % 2)

    def blocks_for(s):
        far = (s + shards // 2) % shards
        order = [lax.dynamic_index_in_dim(new_block, o, 0, keepdims=False) for o in (far, s)]
        return jnp.concatenate(order)

    pick_tab = jnp.stack([blocks_for(me), blocks_for(pair)])

    moments = jnp.stack([first_old, second_old]).astype(bf16)
    params = param_old[None]
    kept, sent = pick(pick_tab, inputs)

    parts = 4
    group = 2 * cap // parts
    tile = (own_rows, width)
    slot = jax.ShapeDtypeStruct((own_rows, cap, width), f32)
    V = pltpu.VMEM

    def state(count):
        wide = (own_rows, count, width)
        return [V((2,) + wide, bf16), V((1,) + wide, bf16)]

    def dma(*shape):
        return pltpu.SemaphoreType.DMA(shape + (2,))

    outs = pl.pallas_call(
        fused_kernel,
        out_shape=(slot, slot, slot, jax.ShapeDtypeStruct((shards, own_rows, cap, width), bf16)),
        in_specs=[pl.BlockSpec(memory_space=pltpu.VMEM)] * 9,
        out_specs=(pl.BlockSpec(memory_space=pltpu.VMEM),) * 4,
        scratch_shapes=[
            V((shards, rows, width), bf16),
            V(kept.shape, bf16),
            V((shards, rows, width), f32), V((shards, rows, width), f32), V((shards, rows, width), f32),
            V((2, rows, width), bf16),
            V((parts, group, 2, 2, 2) + tile, f32),
            V((parts, group, 2, 2) + tile, f32),
            V((parts, group, 2) + tile, f32),
            V((parts, group, 2) + tile, bf16), V((parts, group, 2) + tile, bf16),
            V((parts, group) + tile, f32),
            V((parts, group) + tile, bf16), V((parts, group) + tile, bf16),
            V((parts // 2, group) + tile, f32),
            V((parts // 2, group) + tile, bf16), V((parts // 2, group) + tile, bf16),
            *state(old_cap), *state(old_cap),
            *state(2 * cap), *state(cap), *state(2 * cap), *state(cap),
            V((2, own_rows, cap, width), bf16), V((1, own_rows, cap, width), f32),
            V((own_rows, cap, width), f32),
            V((own_rows, cap, width), bf16),
            dma(shards), dma(), dma(shards), dma(), dma(parts), dma(parts), dma(parts), dma(parts),
            dma(2, 2), dma(parts // 2, shards, 2),
        ],
        compiler_params=pltpu.CompilerParams(
            collective_id=0, has_side_effects=True, vmem_limit_bytes=63 << 20
        ),
    )(hot, queries, keys, grad_out, kept, sent, moments, params.astype(bf16), params)
    every = outs[3].transpose(1, 0, 2, 3).reshape(own_rows, blocks, width)
    weights = spread(new_slot[:, None] == jnp.arange(blocks)[None, :], every)
    return tuple(outs[:3]) + (weights,)


def solution(mesh):
    placed = (
        P(("rep", "shard"), None),
        P(("rep", "shard"), None),
        P(("rep", "shard"), None),
        P(("rep", "shard"), None),
        P(),
        P(),
        P("rep", "shard", None),
        P("rep", "shard", None),
        P("rep", "shard", None),
    )
    small = mesh.shape["shard"] == 4 and mesh.shape["rep"] == 8
    return jax.shard_map(
        fused if small else local,
        mesh=mesh,
        in_specs=placed,
        out_specs=(
            P("rep", "shard", None),
            P("rep", "shard", None),
            P("rep", "shard", None),
            P("rep", None, None),
        ),
        check_vma=False,
    )
```

```python
import jax
import jax.numpy as jnp
from jax import lax
from jax.experimental import pallas as pl
from jax.experimental.pallas import tpu as pltpu
from jax.sharding import PartitionSpec as P

KV = 4
HD = 128
GRP = 8
STEP = 1000

beta_first = 0.9
beta_second = 0.95
learning_rate = 0.02
decay_rate = 0.1
epsilon = 1e-08


def owner_ranks(owner, owners):
    onehot = (owner[:, None] == jnp.arange(owners, dtype=jnp.int32)[None, :]).astype(jnp.int32)
    running = jnp.cumsum(onehot, axis=0)
    return jnp.sum(running * onehot, axis=1) - 1


def adamw(param, first, second, gradient):
    first = beta_first * first + (1.0 - beta_first) * gradient
    second = beta_second * second + (1.0 - beta_second) * gradient * gradient
    first_hat = first / (1.0 - beta_first**STEP)
    second_hat = second / (1.0 - beta_second**STEP)
    param = param - learning_rate * (
        first_hat / (jnp.sqrt(second_hat) + epsilon) + decay_rate * param
    )
    return (param, first, second)


def value_kernel(where_ref, q_ref, k_ref, g_ref, o_ref):
    me = where_ref[0]
    rows = q_ref.shape[0]
    length = k_ref.shape[0]
    row = lax.broadcasted_iota(jnp.int32, (rows, length), 0)
    col = lax.broadcasted_iota(jnp.int32, (rows, length), 1)
    allowed = col <= jnp.where(col < rows, row, (me + 1) * rows - 1)
    keys = k_ref[...]
    total = jnp.zeros((length, HD), jnp.float32)
    for h in range(GRP):
        span = slice(h * HD, (h + 1) * HD)
        scores = lax.dot_general(
            q_ref[:, span], keys, (((1,), (1,)), ((), ())), preferred_element_type=jnp.float32
        ) * HD ** (-0.5)
        scores = jnp.where(allowed, scores, -jnp.inf)
        highest = jnp.max(scores, axis=-1, keepdims=True)
        weights = jnp.exp(scores - highest)
        probs = (weights / jnp.sum(weights, axis=-1, keepdims=True)).astype(jnp.bfloat16)
        total = total + lax.dot_general(
            probs, g_ref[:, span], (((0,), (0,)), ((), ())), preferred_element_type=jnp.float32
        )
    o_ref[...] = total


def value_terms(me, queries, keys_all, grad_out):
    rows = queries.shape[0]
    length = keys_all.shape[0]
    return pl.pallas_call(
        value_kernel,
        grid=(KV,),
        out_shape=jax.ShapeDtypeStruct((length, KV * HD), jnp.float32),
        in_specs=[
            pl.BlockSpec(memory_space=pltpu.SMEM),
            pl.BlockSpec((rows, GRP * HD), lambda g: (0, g)),
            pl.BlockSpec((length, HD), lambda g: (0, g)),
            pl.BlockSpec((rows, GRP * HD), lambda g: (0, g)),
        ],
        out_specs=pl.BlockSpec((length, HD), lambda g: (0, g)),
        cost_estimate=pl.CostEstimate(
            flops=4 * rows * length * HD * GRP * KV, bytes_accessed=4 << 20, transcendentals=0
        ),
    )(me[None], queries, keys_all, grad_out)


def pick_kernel(block_ref, x_ref, o_ref, p_ref):
    width = HD
    count = o_ref.shape[1] // width

    @pl.loop(0, count)
    def _(i):
        into = pl.ds(pl.multiple_of(i * width, width), width)
        o_ref[:, into] = x_ref[:, pl.ds(pl.multiple_of(block_ref[0, i] * width, width), width)]
        p_ref[:, into] = x_ref[:, pl.ds(pl.multiple_of(block_ref[1, i] * width, width), width)]


def pick(blocks, inputs):
    rows, wide = inputs.shape
    half = jax.ShapeDtypeStruct((rows, wide // 2), inputs.dtype)
    return pl.pallas_call(
        pick_kernel,
        out_shape=(half, half),
        in_specs=[
            pl.BlockSpec(memory_space=pltpu.SMEM),
            pl.BlockSpec(memory_space=pltpu.VMEM),
        ],
        out_specs=(pl.BlockSpec(memory_space=pltpu.VMEM),) * 2,
        cost_estimate=pl.CostEstimate(flops=0, bytes_accessed=4 << 20, transcendentals=0),
    )(blocks, inputs)


def swap(x, axis, size, bit):
    return lax.ppermute(x, axis, [(i, i ^ bit) for i in range(size)])


def halve(x, axis, bit_value):
    mine = lax.dynamic_index_in_dim(x, bit_value, axis, keepdims=False)
    other = lax.dynamic_index_in_dim(x, 1 - bit_value, axis, keepdims=False)
    return mine, other


def spread(onehot, state):
    return jnp.einsum(
        "ns,rsc->rnc",
        onehot.astype(state.dtype),
        state,
        precision=lax.Precision.HIGHEST if state.dtype == jnp.float32 else None,
        preferred_element_type=state.dtype,
    )


def moved_state(state, source_owner, source_rank, me, shards, sources, new_capacity):
    old_capacity = state.shape[1]
    rank_hot = source_rank[:, None] == jnp.arange(old_capacity)[None, :]
    mine = spread(rank_hot & (source_owner == me)[:, None], state)

    def my_part(x, first_shard, count):
        at = jnp.clip(me - first_shard, 0, count - 1) * new_capacity
        part = lax.dynamic_slice_in_dim(x, at, new_capacity, axis=1)
        inside = (me >= first_shard) & (me < first_shard + count)
        return jnp.where(inside, part, jnp.zeros_like(part))

    result = my_part(mine, 0, shards)

    def chain(route):
        out = jnp.zeros_like(result)
        come = None
        for step, (sender, receiver, low, high) in enumerate(route):
            count = high - low
            if step == 0 and old_capacity < count * new_capacity:
                raw = lax.ppermute(state, "shard", [(sender, receiver)])
                come = spread(
                    (rank_hot & (source_owner == sender)[:, None])[
                        low * new_capacity : high * new_capacity
                    ],
                    raw,
                )
            else:
                pay = mine[:, low * new_capacity : high * new_capacity]
                if come is not None:
                    skip = (low - before) * new_capacity
                    pay = pay + come[:, skip : skip + count * new_capacity]
                come = lax.ppermute(pay, "shard", [(sender, receiver)])
            before = low
            here = receiver - low
            part = come[:, here * new_capacity : (here + 1) * new_capacity]
            out = out + jnp.where(me == receiver, part, jnp.zeros_like(part))
        return out

    right = chain([(l, l + 1, l + 1, shards) for l in range(shards - 1)])
    left = chain([(l, l - 1, 0, l) for l in range(sources - 1, 0, -1)])
    return result + right + left


def local(queries, keys, grad_out, inputs, old_owner, new_owner, param_old, first_old, second_old):
    shards = lax.axis_size("shard")
    replicas = lax.axis_size("rep")
    me = lax.axis_index("shard")
    rep = lax.axis_index("rep")
    rows = queries.shape[0]
    blocks = old_owner.shape[0]
    block_rows = inputs.shape[1] // blocks
    own_rows = block_rows // replicas
    new_capacity = blocks // shards
    columns = KV * HD
    sources = shards - shards // 4
    bf16 = jnp.bfloat16

    chunks = [keys]
    for k in range(1, shards):
        chunks.append(lax.ppermute(keys, "shard", [(s, s + k) for s in range(shards - k)]))

    new_slot = new_owner * new_capacity + owner_ranks(new_owner, shards)
    match = new_slot[None, :] == jnp.arange(blocks, dtype=jnp.int32)[:, None]

    def by_slot(table):
        return jnp.sum(jnp.where(match, table[None, :], 0), axis=1)

    new_block = by_slot(jnp.arange(blocks, dtype=jnp.int32))
    source_owner = by_slot(old_owner)
    source_rank = by_slot(owner_ranks(old_owner, shards))

    parity = me % 2
    halves = new_block.reshape(shards // 2, 2, new_capacity).transpose(1, 0, 2).reshape(2, -1)
    mine_first = jnp.where(parity == 0, halves, halves[::-1])
    kept, sent = pick(mine_first, inputs)
    arrived = swap(sent, "shard", shards, 1)

    moved = [
        moved_state(x, source_owner, source_rank, me, shards, sources, new_capacity)
        for x in (first_old.astype(bf16), second_old.astype(bf16), param_old)
    ]
    first, second, param = (x.astype(jnp.float32) for x in moved)

    part = value_terms(me, queries, jnp.concatenate(chunks, axis=0), grad_out)
    values = part[:rows]
    for k in range(1, shards):
        values = values + lax.ppermute(
            part[k * rows : (k + 1) * rows], "shard", [(s, s - k) for s in range(k, shards)]
        )
    values = values.astype(bf16)
    values_pair = swap(values, "shard", shards, 1)

    contract = (((0,), (0,)), ((), ()))
    product = lax.dot_general(
        jnp.concatenate([kept, arrived], axis=0),
        jnp.concatenate([values, values_pair], axis=0),
        contract,
        preferred_element_type=jnp.float32,
    )
    bits = [1 << n for n in range(replicas.bit_length() - 1)]
    split = tuple(2 for _ in bits)
    product = product.reshape((-1,) + split + (own_rows, columns))

    def scatter(x, order):
        left = sorted(order, reverse=True)
        for bit in order:
            mine, other = halve(x, 1 + left.index(bit), (rep // bit) % 2)
            x = mine + swap(other.astype(bf16), "rep", replicas, bit).astype(jnp.float32)
            left.remove(bit)
        return x

    mine, other = halve(product, len(bits), rep % 2)
    product = mine + swap(other.astype(bf16), "rep", replicas, 1).astype(jnp.float32)
    product = product.reshape((2, -1) + product.shape[1:])
    a = scatter(product[0], bits[1:])
    b = scatter(product[1], bits[:0:-1])
    gradient = jnp.concatenate([a, b], axis=0).reshape(
        shards // 2, new_capacity, own_rows, columns
    )
    pair = me // 2
    total = lax.dynamic_index_in_dim(gradient, pair, 0, keepdims=False)
    for k in range(1, shards // 2):
        out = lax.dynamic_index_in_dim(gradient, (pair + k) % (shards // 2), 0, keepdims=False)
        total = total + lax.ppermute(
            out.astype(bf16), "shard", [(s, (s + 2 * k) % shards) for s in range(shards)]
        ).astype(jnp.float32)
    gradient = total.transpose(1, 0, 2)

    param_new, first_new, second_new = adamw(param, first, second, gradient)
    working = param_new.astype(bf16)
    every = [working]
    for k in range(1, shards):
        every.append(
            lax.ppermute(working, "shard", [(s, (s + k) % shards) for s in range(shards)])
        )
    stacked = jnp.concatenate(every, axis=1)
    at = ((me - new_slot // new_capacity) % shards) * new_capacity + new_slot % new_capacity
    weights = spread(at[:, None] == jnp.arange(blocks)[None, :], stacked)
    return (param_new, first_new, second_new, weights)


def fused_kernel(
    hot, q_ref, key_ref, g_ref, x_own, x_out, mom_in, par_in, par_full,
    pn_ref, fn_ref, sn_ref, wall,
    kbuf, x_in, part, v_in, v_out, v_pair,
    prod, core_in, keep1, out1, in1, keep2, out2, in2, gown, out3, in3,
    raw_a_mom, raw_a_par, raw_b_mom, raw_b_par,
    a_mom, a_par, b_mom, b_par, r_mom, r_par, l_mom, l_par, st_mom, st_par, grad, w_out,
    k_sem, x_sem, v_sem, vp_sem, c_sem, s1_sem, s2_sem, s3_sem, st_sem, w_sem,
):
    bf16, f32 = jnp.bfloat16, jnp.float32
    me, rep = lax.axis_index("shard"), lax.axis_index("rep")
    shards = kbuf.shape[0]
    rows = key_ref.shape[0]
    length = shards * rows
    sources = shards - shards // 4
    cap = pn_ref.shape[1]
    parts, group = prod.shape[0], prod.shape[1]
    core, xbit, ybit = rep % 2, (rep // 2) % 2, (rep // 4) % 2
    pair = me + 1 - 2 * (me % 2)
    cross = (me + shards // 2) % shards
    rep_core = rep + 1 - 2 * core
    rep_x = rep + 2 - 4 * xbit
    rep_y = rep + 4 - 8 * ybit
    has_left, has_right = me > 0, me < shards - 1

    def send(src, dst, sem, target):
        return pltpu.make_async_remote_copy(
            src_ref=src, dst_ref=dst, send_sem=sem.at[0], recv_sem=sem.at[1],
            device_id=target, device_id_type=pl.DeviceIdType.MESH,
        )

    left, right = (rep, me - 1), (rep, me + 1)

    barrier = pltpu.get_barrier_semaphore()

    def greet(target):
        pl.semaphore_signal(barrier, inc=1, device_id=target, device_id_type=pl.DeviceIdType.MESH)

    for target in ((rep_core, me), (rep_x, me), (rep_y, me), (rep, cross)):
        greet(target)
    pl.when(has_left)(lambda: greet(left))
    pl.when(has_right)(lambda: greet(right))
    pl.semaphore_wait(barrier, 5 + jnp.where(has_left & has_right, 1, 0))

    def key_copy(j):
        src = key_ref if j == 0 else kbuf.at[j]
        return send(src, kbuf.at[j + 1], k_sem.at[j], right)

    own = (mom_in, par_in)
    raw_buf = ((raw_a_mom, raw_a_par), (raw_b_mom, raw_b_par))
    a_buf, b_buf = (a_mom, a_par), (b_mom, b_par)
    r_buf, l_buf = (r_mom, r_par), (l_mom, l_par)
    st_buf = (st_mom, st_par)

    def raw(kind, direction):
        return send(
            own[kind], raw_buf[direction][kind], st_sem.at[kind, direction], (right, left)[direction]
        )

    def raw_send(kind):
        pl.when(me == 0)(lambda: raw(kind, 0).start())
        pl.when(me == sources - 1)(lambda: raw(kind, 1).start())

    pl.when(has_right)(lambda: key_copy(0).start())
    raw_send(0)

    x_copy = send(x_out, x_in, x_sem, (rep, pair))
    x_copy.start()

    kbuf[0] = key_ref[...]
    for j in range(1, shards):
        @pl.when(me >= j)
        def _(j=j):
            key_copy(j - 1).wait_recv()
            if j < shards - 1:
                pl.when(has_right)(lambda: key_copy(j).start())

        @pl.when(me < j)
        def _(j=j):
            kbuf[j] = jnp.zeros(kbuf.shape[1:], kbuf.dtype)

    row = lax.broadcasted_iota(jnp.int32, (rows, length), 0)
    col = lax.broadcasted_iota(jnp.int32, (rows, length), 1)
    allowed = col <= jnp.where(col < rows, row, (me + 1) * rows - 1)

    @pl.loop(0, KV)
    def _(g):
        at = pl.ds(pl.multiple_of(g * HD, HD), HD)
        keys = kbuf[:, :, at].reshape(length, HD)
        total = jnp.zeros((length, HD), f32)
        for h in range(GRP):
            span = pl.ds(pl.multiple_of(g * (GRP * HD) + h * HD, HD), HD)
            scores = lax.dot_general(
                q_ref[:, span], keys, (((1,), (1,)), ((), ())), preferred_element_type=f32
            ) * HD ** (-0.5)
            scores = jnp.where(allowed, scores, -jnp.inf)
            highest = jnp.max(scores, axis=-1, keepdims=True)
            weights = jnp.exp(scores - highest)
            probs = (weights / jnp.sum(weights, axis=-1, keepdims=True)).astype(bf16)
            total = total + lax.dot_general(
                probs, g_ref[:, span], (((0,), (0,)), ((), ())), preferred_element_type=f32
            )
        part[:, :, at] = total.reshape(shards, rows, HD)

    def select(kind, out, first, count, sources_of, extra=None):
        kinds = own[kind].shape[0]
        tables = []
        for which, ref in sources_of:
            tables.append(hot[which, pl.ds(first, count)].astype(ref.dtype))

        @pl.loop(0, own[kind].shape[1])
        def _(r):
            for m in range(kinds):
                total = None
                for table, (_, ref) in zip(tables, sources_of):
                    term = jnp.dot(
                        table, ref[m, r], preferred_element_type=f32,
                        precision=lax.Precision.HIGHEST if ref.dtype == f32 else None,
                    )
                    total = term if total is None else total + term
                if extra is not None:
                    total = total + extra(m, r).astype(f32)
                out[m, r] = total.astype(out.dtype)

    def forward_copy(kind, role):
        if role == 0:
            return send(r_buf[kind], a_buf[kind], st_sem.at[kind, 0], right)
        if role == 1:
            return send(l_buf[kind], b_buf[kind], st_sem.at[kind, 1], left)
        return send(l_buf[kind], b_buf[kind], st_sem.at[kind, 0], right)

    def forward_right(kind):
        @pl.when(me == 1)
        def _():
            raw(kind, 0).wait_recv()
            far = (1, raw_buf[0][kind])
            select(kind, r_buf[kind], 2 * cap, 2 * cap, [(0, own[kind]), far])
            forward_copy(kind, 0).start()

    def forward_left(kind):
        @pl.when(me == 1)
        def _():
            raw(kind, 1).wait_recv()
            far = (2, raw_buf[1][kind])
            select(kind, l_buf[kind], 0, cap, [(0, own[kind]), far])
            forward_copy(kind, 1).start()

    def forward_last(kind):
        @pl.when(me == 2)
        def _():
            forward_copy(kind, 0).wait_recv()
            select(
                kind, l_buf[kind], 3 * cap, cap, [(0, own[kind])],
                lambda m, r: a_buf[kind][m, r, pl.ds(cap, cap)],
            )
            forward_copy(kind, 2).start()

    forward_right(0)

    def v_copy(d):
        return send(v_out.at[d], v_in.at[d], v_sem.at[d], left)

    for d in range(shards):
        pl.when((me >= d) & has_right)(lambda d=d: v_copy(d).wait_recv())

        @pl.when((me >= d) & has_right)
        def _(d=d):
            v_out[d] = part[me - d] + v_in[d]

        @pl.when((me >= d) & jnp.logical_not(has_right))
        def _(d=d):
            v_out[d] = part[me - d]

        pl.when(me > d)(lambda d=d: v_copy(d).start())

        @pl.when(me == d)
        def _(d=d):
            v_pair[0] = v_out[d].astype(bf16)

    vp_copy = send(v_pair.at[0], v_pair.at[1], vp_sem, (rep, pair))
    vp_copy.start()
    raw_send(1)

    def settle(kind):
        mine = (0, (mom_in, par_full)[kind])

        @pl.when(me == 0)
        def _():
            forward_copy(kind, 1).wait_recv()
            select(kind, st_buf[kind], 0, cap, [mine], lambda m, r: b_buf[kind][m, r])

        @pl.when(me == 1)
        def _():
            far = [(1, raw_buf[0][kind]), (2, raw_buf[1][kind])]
            select(kind, st_buf[kind], cap, cap, [mine] + far)

        @pl.when(me == 2)
        def _():
            select(
                kind, st_buf[kind], 2 * cap, cap, [mine],
                lambda m, r: a_buf[kind][m, r, pl.ds(0, cap)],
            )

        @pl.when(me == 3)
        def _():
            forward_copy(kind, 2).wait_recv()
            select(kind, st_buf[kind], 3 * cap, cap, [mine], lambda m, r: b_buf[kind][m, r])

    vp_copy.wait_recv()
    x_copy.wait_recv()
    contract = (((0,), (0,)), ((), ()))

    def core_copy(n):
        return send(prod.at[n, :, :, :, 1 - core], core_in.at[n], c_sem.at[n], (rep_core, me))

    for n in range(parts):
        @pl.loop(0, group)
        def _(i, n=n):
            at = pl.ds(pl.multiple_of((n * group + i) * HD, HD), HD)
            block = lax.dot_general(x_own[:, at], v_pair[0], contract, preferred_element_type=f32)
            block += lax.dot_general(x_in[:, at], v_pair[1], contract, preferred_element_type=f32)
            prod[n, i] = block.reshape(prod.shape[2:])

        core_copy(n).start()

    forward_left(0)

    def first_copy(n):
        return send(out1.at[n], in1.at[n], s1_sem.at[n], ((rep_x, rep_y)[n % 2], me))

    def second_copy(n):
        return send(out2.at[n], in2.at[n], s2_sem.at[n], ((rep_y, rep_x)[n % 2], me))

    def cross_copy(n):
        return send(out3.at[n], in3.at[n], s3_sem.at[n], (rep, cross))

    for n in range(parts):
        core_copy(n).wait_recv()

        @pl.loop(0, group)
        def _(i, n=n):
            if n % 2 == 0:
                out1[n, i] = (prod[n, i, :, 1 - xbit, core] + core_in[n, i, :, 1 - xbit]).astype(bf16)
                keep1[n, i] = prod[n, i, :, xbit, core] + core_in[n, i, :, xbit]
            else:
                out1[n, i] = (prod[n, i, 1 - ybit, :, core] + core_in[n, i, 1 - ybit]).astype(bf16)
                keep1[n, i] = prod[n, i, ybit, :, core] + core_in[n, i, ybit]

        first_copy(n).start()

    forward_right(1)

    for n in range(parts):
        first_copy(n).wait_recv()
        bit = (ybit, xbit)[n % 2]

        @pl.loop(0, group)
        def _(i, n=n, bit=bit):
            out2[n, i] = (keep1[n, i, 1 - bit] + in1[n, i, 1 - bit].astype(f32)).astype(bf16)
            keep2[n, i] = keep1[n, i, bit] + in1[n, i, bit].astype(f32)

        second_copy(n).start()

    forward_left(1)
    forward_last(0)

    half = parts // 2
    for n in range(parts):
        second_copy(n).wait_recv()

        @pl.loop(0, group)
        def _(i, n=n):
            total = keep2[n, i] + in2[n, i].astype(f32)
            if n < half:
                out3[n, i] = total.astype(bf16)
            else:
                gown[n - half, i] = total

        if n < half:
            cross_copy(n).start()

    forward_last(1)
    for kind in range(2):
        settle(kind)

    wrows = wall.shape[1] // half

    def w_copy(n, t, direction):
        origin = (me - t, me + t)[direction]
        ref = wall.at[origin, pl.ds(n * wrows, wrows)]
        src = w_out.at[pl.ds(n * wrows, wrows)] if t == 0 else ref
        return send(src, ref, w_sem.at[n, t, direction], (right, left)[direction])

    for n in range(half):
        cross_copy(n).wait_recv()

        @pl.loop(0, group)
        def _(i, n=n):
            total = gown[n, i] + in3[n, i].astype(f32)
            grad[:, pl.ds(n * group + i, 1), :] = total[:, None, :]

    for n in range(half):
        @pl.loop(n * wrows, (n + 1) * wrows)
        def _(r):
            param, first, second = adamw(
                st_par[0, r], st_mom[0, r].astype(f32), st_mom[1, r].astype(f32), grad[r]
            )
            pn_ref[r] = param
            fn_ref[r] = first
            sn_ref[r] = second
            w_out[r] = param.astype(bf16)
            wall[me, r] = param.astype(bf16)

        pl.when(has_right)(lambda n=n: w_copy(n, 0, 0).start())
        pl.when(has_left)(lambda n=n: w_copy(n, 0, 1).start())

    for t in range(1, shards):
        for n in range(half):
            @pl.when(me >= t)
            def _(n=n, t=t):
                w_in = wall.at[me - t, pl.ds(n * wrows, wrows)]
                send(w_in, w_in, w_sem.at[n, t - 1, 0], right).wait_recv()
                if t < shards - 1:
                    pl.when(has_right)(lambda: w_copy(n, t, 0).start())

            @pl.when(me + t < shards)
            def _(n=n, t=t):
                w_in = wall.at[me + t, pl.ds(n * wrows, wrows)]
                send(w_in, w_in, w_sem.at[n, t - 1, 1], left).wait_recv()
                if t < shards - 1:
                    pl.when(has_left)(lambda: w_copy(n, t, 1).start())

    for j in range(shards - 1):
        pl.when(has_right & (me >= j))(lambda j=j: key_copy(j).wait_send())
    for kind in range(2):
        pl.when(me == 0)(lambda kind=kind: raw(kind, 0).wait_send())
        pl.when(me == sources - 1)(lambda kind=kind: raw(kind, 1).wait_send())
        pl.when(me == 1)(lambda kind=kind: forward_copy(kind, 0).wait_send())
        pl.when(me == 1)(lambda kind=kind: forward_copy(kind, 1).wait_send())
        pl.when(me == 2)(lambda kind=kind: forward_copy(kind, 2).wait_send())
    x_copy.wait_send()
    vp_copy.wait_send()
    for d in range(shards):
        pl.when(me > d)(lambda d=d: v_copy(d).wait_send())
    for n in range(parts):
        core_copy(n).wait_send()
        first_copy(n).wait_send()
        second_copy(n).wait_send()
        if n < half:
            cross_copy(n).wait_send()
    for n in range(half):
        for t in range(shards - 1):
            pl.when(has_right & (me >= t))(lambda n=n, t=t: w_copy(n, t, 0).wait_send())
            pl.when(has_left & (me + t < shards))(lambda n=n, t=t: w_copy(n, t, 1).wait_send())


def fused(queries, keys, grad_out, inputs, old_owner, new_owner, param_old, first_old, second_old):
    shards = lax.axis_size("shard")
    replicas = lax.axis_size("rep")
    me = lax.axis_index("shard")
    rows = queries.shape[0]
    blocks = old_owner.shape[0]
    own_rows = inputs.shape[1] // blocks // replicas
    cap = blocks // shards
    width = KV * HD
    old_cap = param_old.shape[1]
    bf16, f32 = jnp.bfloat16, jnp.float32

    new_slot = new_owner * cap + owner_ranks(new_owner, shards)
    match = new_slot[None, :] == jnp.arange(blocks, dtype=jnp.int32)[:, None]
    old_rank = owner_ranks(old_owner, shards)

    def by_slot(table):
        return jnp.sum(jnp.where(match, table[None, :], 0), axis=1)

    new_block = by_slot(jnp.arange(blocks, dtype=jnp.int32)).reshape(shards, cap)
    owner = by_slot(old_owner)
    rank = by_slot(old_rank)
    rank_hot = rank[:, None] == jnp.arange(old_cap)[None, :]
    hot = jnp.stack(
        [rank_hot & (owner == o)[:, None] for o in (me, 0, shards - shards // 4 - 1)]
    ).astype(f32)
    pair = me + 1 - 2 * (me % 2)

    def blocks_for(s):
        far = (s + shards // 2) % shards
        order = [lax.dynamic_index_in_dim(new_block, o, 0, keepdims=False) for o in (far, s)]
        return jnp.concatenate(order)

    pick_tab = jnp.stack([blocks_for(me), blocks_for(pair)])

    moments = jnp.stack([first_old, second_old]).astype(bf16)
    params = param_old[None]
    kept, sent = pick(pick_tab, inputs)

    parts = 4
    group = 2 * cap // parts
    tile = (own_rows, width)
    slot = jax.ShapeDtypeStruct((own_rows, cap, width), f32)
    V = pltpu.VMEM

    def state(count):
        wide = (own_rows, count, width)
        return [V((2,) + wide, bf16), V((1,) + wide, bf16)]

    def dma(*shape):
        return pltpu.SemaphoreType.DMA(shape + (2,))

    outs = pl.pallas_call(
        fused_kernel,
        out_shape=(slot, slot, slot, jax.ShapeDtypeStruct((shards, own_rows, cap, width), bf16)),
        in_specs=[pl.BlockSpec(memory_space=pltpu.VMEM)] * 9,
        out_specs=(pl.BlockSpec(memory_space=pltpu.VMEM),) * 4,
        scratch_shapes=[
            V((shards, rows, width), bf16),
            V(kept.shape, bf16),
            V((shards, rows, width), f32), V((shards, rows, width), f32), V((shards, rows, width), f32),
            V((2, rows, width), bf16),
            V((parts, group, 2, 2, 2) + tile, f32),
            V((parts, group, 2, 2) + tile, f32),
            V((parts, group, 2) + tile, f32),
            V((parts, group, 2) + tile, bf16), V((parts, group, 2) + tile, bf16),
            V((parts, group) + tile, f32),
            V((parts, group) + tile, bf16), V((parts, group) + tile, bf16),
            V((parts // 2, group) + tile, f32),
            V((parts // 2, group) + tile, bf16), V((parts // 2, group) + tile, bf16),
            *state(old_cap), *state(old_cap),
            *state(2 * cap), *state(cap), *state(2 * cap), *state(cap),
            V((2, own_rows, cap, width), bf16), V((1, own_rows, cap, width), f32),
            V((own_rows, cap, width), f32),
            V((own_rows, cap, width), bf16),
            dma(shards), dma(), dma(shards), dma(), dma(parts), dma(parts), dma(parts), dma(parts),
            dma(2, 2), dma(parts // 2, shards, 2),
        ],
        compiler_params=pltpu.CompilerParams(
            collective_id=0, has_side_effects=True, vmem_limit_bytes=63 << 20
        ),
    )(hot, queries, keys, grad_out, kept, sent, moments, params.astype(bf16), params)
    every = outs[3].transpose(1, 0, 2, 3).reshape(own_rows, blocks, width)
    weights = spread(new_slot[:, None] == jnp.arange(blocks)[None, :], every)
    return tuple(outs[:3]) + (weights,)


def solution(mesh):
    placed = (
        P(("rep", "shard"), None),
        P(("rep", "shard"), None),
        P(("rep", "shard"), None),
        P(("rep", "shard"), None),
        P(),
        P(),
        P("rep", "shard", None),
        P("rep", "shard", None),
        P("rep", "shard", None),
    )
    small = mesh.shape["shard"] == 4 and mesh.shape["rep"] == 8
    return jax.shard_map(
        fused if small else local,
        mesh=mesh,
        in_specs=placed,
        out_specs=(
            P("rep", "shard", None),
            P("rep", "shard", None),
            P("rep", "shard", None),
            P("rep", None, None),
        ),
        check_vma=False,
    )
```
